32 devices in a mesh: dom: 8 (over z, y), col: 4 (over x, core).
Axes of the slice: x: 2, y: 2, z: 4, core: 2. Of those that a mesh axis runs over, the one named last changes fastest.
Arguments:
- margin: bfloat16 [64, 27, 128, 128], P(('dom', 'col')), may hold values from -0.05 to 1.05
- neighbours: int32 [64, 27], P('dom'), may hold values from 0 to 9, as said below
- pattern: int32 [64, 27], P('dom'), may hold values from 0 to 1, as said below
- colour: int32 [64], replicated, may hold values from 0 to 3
- send_list: int32 [8, 2, 1], replicated, may hold values from 0 to 7
Outputs:
- probe_images: float32 [8192, 512], P('dom', 'col')
The draws below stay inside these ranges and needn't reach their ends.
Inputs may be any that keep to these rules, and one draw needn't show every extreme that they name: `neighbours`: slot 13 of every block row names the block itself. `pattern`: slot 13 of every block row is present.
All inputs are finite; a program needn't handle non-finite values.
Results may differ from the reference program's by a relative error of at most 0.0011.
Values may be sent and summed in bfloat16 or wider, within the bound.
No kernel may reach another device: no remote copies, remote signals or barrier semaphores. Data moves between devices by JAX's collectives and lax.ppermute only.
A program may use at most 128 MiB of HBM per device.

```python
import math
import jax
import jax.numpy as jnp
from jax import lax

CLUSTER_ORBITALS = 128
NEIGHBOUR_SLOTS = 27
COLOURS = 4
DOMAIN_BLOCKS = 8
BORDER_BLOCKS = 1
TOTAL_BLOCKS = 64
N_DOM = 8


def draw_margin(key, part):
    array_extent = (TOTAL_BLOCKS, NEIGHBOUR_SLOTS, CLUSTER_ORBITALS, CLUSTER_ORBITALS)
    block_values = 0.008 * jax.random.truncated_normal(key, -5.0, 5.0, array_extent, jnp.float32)
    middle_position = (jnp.arange(NEIGHBOUR_SLOTS) == 13).astype(jnp.float32)
    identity = jnp.eye(CLUSTER_ORBITALS, dtype=jnp.float32)
    return (block_values + middle_position[None, :, None, None] * identity[None, None, :, :]).astype(jnp.bfloat16)


def draw_neighbours(key, part):
    block_values = jax.random.randint(key, (TOTAL_BLOCKS, NEIGHBOUR_SLOTS), 0, DOMAIN_BLOCKS + 2 * BORDER_BLOCKS, dtype=jnp.int32)
    itself = (jnp.arange(TOTAL_BLOCKS, dtype=jnp.int32) % DOMAIN_BLOCKS)[:, None]
    middle_position = (jnp.arange(NEIGHBOUR_SLOTS, dtype=jnp.int32) == 13)[None, :]
    return jnp.where(middle_position, itself, block_values).astype(jnp.int32)


def draw_pattern(key, part):
    block_values = jax.random.randint(key, (TOTAL_BLOCKS, NEIGHBOUR_SLOTS), 0, 6, dtype=jnp.int32)
    present = (block_values != 0).astype(jnp.int32)
    middle_position = (jnp.arange(NEIGHBOUR_SLOTS, dtype=jnp.int32) == 13)[None, :]
    return jnp.where(middle_position, 1, present).astype(jnp.int32)


def with_ends(values, key, smallest, top_value):
    extent = values.shape
    spot = [jax.random.randint(jax.random.fold_in(key, axis), (), 0, extent[axis]) for axis in range(len(extent))]
    values = values.at[tuple(spot)].set(smallest)
    longest = extent.index(max(extent))
    spot[longest] = (spot[longest] + 1) % extent[longest]
    return values.at[tuple(spot)].set(top_value)


def setup_inputs(seed: int = 0) -> dict:
    seeds = jax.random.split(jax.random.key(seed), 6)
    return {
        "margin": draw_margin(jax.random.fold_in(seeds[5], 71), 0),
        "neighbours": draw_neighbours(jax.random.fold_in(seeds[5], 71), 0),
        "pattern": draw_pattern(jax.random.fold_in(seeds[5], 71), 0),
        "colour": with_ends(jax.random.randint(seeds[3], (TOTAL_BLOCKS,), 0, COLOURS), jax.random.fold_in(seeds[3], 1), 0, COLOURS - 1).astype(jnp.int32),
        "send_list": with_ends(jax.random.randint(seeds[4], (N_DOM, 2, BORDER_BLOCKS), 0, DOMAIN_BLOCKS), jax.random.fold_in(seeds[4], 1), 0, DOMAIN_BLOCKS - 1).astype(jnp.int32),
    }


CENTRE = 1.0
HALF_WIDTH = 0.9


def cheb_coefficients():
    samples = []
    for index_k in range(3):
        angle_value = math.pi * (index_k + 0.5) / 3.0
        samples.append((angle_value, (CENTRE + HALF_WIDTH * math.cos(angle_value)) ** -0.5))
    coeffs = []
    for order in range(3):
        coeffs.append(2.0 / 3.0 * sum(value * math.cos(order * angle_value) for angle_value, value in samples))
    coeffs[0] = 0.5 * coeffs[0]
    return coeffs


def global_neighbours(neighbours, send_list):
    domains = jnp.arange(N_DOM, dtype=jnp.int32)
    lower = (domains + N_DOM - 1) % N_DOM
    upper = (domains + 1) % N_DOM
    own_ids = domains[:, None] * DOMAIN_BLOCKS + jnp.arange(DOMAIN_BLOCKS, dtype=jnp.int32)[None, :]
    low_ids = lower[:, None] * DOMAIN_BLOCKS + send_list[lower, 1]
    high_ids = upper[:, None] * DOMAIN_BLOCKS + send_list[upper, 0]
    extended = jnp.concatenate([own_ids, low_ids, high_ids], axis=1).astype(jnp.int32)
    block_domain = (jnp.arange(TOTAL_BLOCKS, dtype=jnp.int32) // DOMAIN_BLOCKS).astype(jnp.int32)
    return extended[block_domain[:, None], neighbours].astype(jnp.int32)


def reference(margin, neighbours, pattern, colour, send_list):
    coeffs = cheb_coefficients()
    global_ids = global_neighbours(neighbours, send_list)
    matrix = margin.astype(jnp.float32)
    live = pattern.astype(jnp.float32)
    identity = jnp.eye(CLUSTER_ORBITALS, dtype=jnp.float32)
    neighbour_colour = colour[global_ids]

    def per_colour(shade):
        hit = (colour == shade).astype(jnp.float32)
        probe = hit[:, None, None] * identity[None, :, :]
        select = live * (neighbour_colour == shade).astype(jnp.float32)
        spread = jnp.einsum('bk,bkij->bij', select, matrix)
        first = ((spread - CENTRE * probe) / HALF_WIDTH).astype(jnp.bfloat16)
        first = lax.optimization_barrier(first).astype(jnp.float32)
        product = jnp.zeros((TOTAL_BLOCKS, CLUSTER_ORBITALS, CLUSTER_ORBITALS), jnp.float32)
        for neighbour_position in range(NEIGHBOUR_SLOTS):
            blocks = matrix[:, neighbour_position] * live[:, neighbour_position, None, None]
            product = product + jnp.einsum('bij,bjl->bil', blocks, first[global_ids[:, neighbour_position]])
        applied = (product - CENTRE * first) / HALF_WIDTH
        second = 2.0 * applied - probe
        return coeffs[0] * probe + coeffs[1] * first + coeffs[2] * second

    images = lax.map(per_colour, jnp.arange(COLOURS, dtype=jnp.int32))
    return images.transpose(1, 2, 0, 3).reshape(TOTAL_BLOCKS * CLUSTER_ORBITALS, COLOURS * CLUSTER_ORBITALS)
```

```python
import functools
import math

import jax
import jax.numpy as jnp
from jax import lax
from jax.experimental import pallas as pl
from jax.experimental.pallas import tpu as pltpu
from jax.sharding import PartitionSpec as P

CENTRE = 1.0
HALF_WIDTH = 0.9
ANY = pl.BlockSpec(memory_space=pl.ANY)
SMEM = pl.BlockSpec(memory_space=pltpu.SMEM)
VMEM = pl.BlockSpec(memory_space=pltpu.VMEM)


def cheb_coefficients():
    samples = []
    for index_k in range(3):
        angle_value = math.pi * (index_k + 0.5) / 3.0
        samples.append((angle_value, (CENTRE + HALF_WIDTH * math.cos(angle_value)) ** (-0.5)))
    coeffs = []
    for order in range(3):
        coeffs.append(
            2.0
            / 3.0
            * sum((value * math.cos(order * angle_value) for angle_value, value in samples))
        )
    coeffs[0] = 0.5 * coeffs[0]
    return coeffs


def first_kernel(
    ndomain, ncolour, neighbours, pattern, colour, send_list, margin, first, blocks, sums, table, sems
):
    domain = lax.axis_index("dom")
    shade = lax.axis_index("col")
    rows, slots = margin.shape[:2]
    own = neighbours.shape[0]
    width = send_list.shape[2]
    copies = [
        pltpu.make_async_copy(margin.at[row], blocks.at[row], sems.at[row]) for row in range(rows)
    ]
    for copy in copies:
        copy.start()
    lower = lax.rem(domain + ndomain - 1, ndomain)
    upper = lax.rem(domain + 1, ndomain)

    @pl.loop(0, own)
    def _(i):
        table[i] = colour[domain * own + i]

    for i in range(width):
        table[own + i] = colour[lower * own + send_list[lower, 1, i]]
        table[own + width + i] = colour[upper * own + send_list[upper, 0, i]]
    sums[...] = jnp.zeros_like(sums)
    orbits = margin.shape[2]
    eye = (
        lax.broadcasted_iota(jnp.int32, (orbits, orbits), 0)
        == lax.broadcasted_iota(jnp.int32, (orbits, orbits), 1)
    ).astype(jnp.float32)
    for row in range(rows):
        block = shade * rows + row
        copies[row].wait()

        @pl.loop(0, slots)
        def _(k):
            live = pattern[block, k] == 1
            where = jnp.where(live, table[neighbours[block, k]], ncolour)
            sums[row, where] += blocks[row, k].astype(jnp.float32)

        sums[row, table[block]] -= CENTRE * eye
        for c in range(ncolour):
            first[row, :, c * orbits : (c + 1) * orbits] = (sums[row, c] / HALF_WIDTH).astype(
                jnp.bfloat16
            )


def first_terms(ndomain, ncolour, neighbours, pattern, colour, send_list, margin):
    rows, slots, orbits, _ = margin.shape
    ext = neighbours.shape[0] + 2 * send_list.shape[2]
    return pl.pallas_call(
        functools.partial(first_kernel, ndomain, ncolour),
        out_shape=jax.ShapeDtypeStruct((rows, orbits, ncolour * orbits), jnp.bfloat16),
        in_specs=[SMEM] * 4 + [ANY],
        out_specs=VMEM,
        scratch_shapes=[
            pltpu.VMEM(margin.shape, jnp.bfloat16),
            pltpu.VMEM((rows, ncolour + 1, orbits, orbits), jnp.float32),
            pltpu.SMEM((ext,), jnp.int32),
            pltpu.SemaphoreType.DMA((rows,)),
        ],
        name="first_terms",
    )(neighbours, pattern, colour, send_list, margin)


def place(entry, shade, rows, own):
    owner = lax.div(entry, rows)
    return jnp.where(entry < own, (owner ^ shade) * rows + lax.rem(entry, rows), entry)


def border_kernel(own, send_list, *refs):
    pieces, (up, down, sems) = refs[:-3], refs[-3:]
    domain = lax.axis_index("dom")
    shade = lax.axis_index("col")
    rows = pieces[0].shape[0]
    copies = []
    for side, out in ((1, up), (0, down)):
        for i in range(send_list.shape[2]):
            entry = send_list[domain, side, i]
            relative = lax.div(entry, rows) ^ shade
            for piece in range(len(pieces)):

                @pl.when(relative == piece)
                def _():
                    pltpu.make_async_copy(
                        pieces[piece].at[lax.rem(entry, rows)], out.at[i], sems.at[side, i]
                    ).start()

            copies.append(pltpu.make_async_copy(pieces[0].at[0], out.at[i], sems.at[side, i]))
    for copy in copies:
        copy.wait()


def borders(own, send_list, pieces):
    shape = jax.ShapeDtypeStruct((send_list.shape[2],) + pieces[0].shape[1:], jnp.bfloat16)
    return pl.pallas_call(
        functools.partial(border_kernel, own),
        out_shape=(shape, shape),
        in_specs=[SMEM] + [ANY] * len(pieces),
        out_specs=(ANY, ANY),
        scratch_shapes=[pltpu.SemaphoreType.DMA((2, send_list.shape[2]))],
        name="borders",
    )(send_list, *pieces)


def image_kernel(coeffs, ncolour, neighbours, pattern, colour, margin, *refs):
    pieces, (images, blocks, ext, sems) = refs[:-4], refs[-4:]
    domain = lax.axis_index("dom")
    shade = lax.axis_index("col")
    rows, slots, orbits, _ = margin.shape
    own = neighbours.shape[0]
    copies = []
    for row in range(rows):
        copies.append(pltpu.make_async_copy(margin.at[row], blocks.at[row], sems.at[row]))
    at = 0
    for i, piece in enumerate(pieces):
        size = piece.shape[0]
        copies.append(
            pltpu.make_async_copy(piece, ext.at[pl.ds(at, size)], sems.at[rows + i])
        )
        at += size
    for copy in copies:
        copy.start()
    ext[at] = jnp.zeros(ext.shape[1:], jnp.bfloat16)
    for copy in copies:
        copy.wait()
    half = 2 * orbits
    eye = (
        lax.broadcasted_iota(jnp.int32, (orbits, orbits), 0)
        == lax.broadcasted_iota(jnp.int32, (orbits, orbits), 1)
    ).astype(jnp.float32)
    for row in range(rows):
        block = shade * rows + row
        mine = colour[domain * own + block]
        spots = []
        for k in range(slots):
            spot = place(neighbours[block, k], shade, rows, own)
            spots.append(jnp.where(pattern[block, k] == 1, spot, at))
        for h in range(ncolour // 2):
            lanes = slice(h * half, (h + 1) * half)
            total = jnp.zeros((orbits, half), jnp.float32)
            for k in range(0, slots, 2):
                ks = range(k, min(k + 2, slots))
                left = jnp.concatenate([blocks[row, j] for j in ks], axis=1)
                right = jnp.concatenate([ext[spots[j], :, lanes] for j in ks], axis=0)
                total += jnp.dot(left, right, preferred_element_type=jnp.float32)
            for c in range(2):
                cut = slice(c * orbits, (c + 1) * orbits)
                first = ext[row, :, h * half + c * orbits : h * half + (c + 1) * orbits]
                first = first.astype(jnp.float32)
                probe = jnp.where(mine == 2 * h + c, eye, 0.0)
                applied = (total[:, cut] - CENTRE * first) / HALF_WIDTH
                images[2 * h + c, row] = (
                    coeffs[0] * probe + coeffs[1] * first + coeffs[2] * (2.0 * applied - probe)
                )


def image_terms(coeffs, ncolour, neighbours, pattern, colour, margin, pieces):
    rows, slots, orbits, _ = margin.shape
    total = sum(piece.shape[0] for piece in pieces)
    return pl.pallas_call(
        functools.partial(image_kernel, coeffs, ncolour),
        out_shape=jax.ShapeDtypeStruct((ncolour, rows, orbits, orbits), jnp.float32),
        in_specs=[SMEM] * 3 + [ANY] * (1 + len(pieces)),
        out_specs=VMEM,
        scratch_shapes=[
            pltpu.VMEM(margin.shape, jnp.bfloat16),
            pltpu.VMEM((total + 1,) + pieces[0].shape[1:], jnp.bfloat16),
            pltpu.SemaphoreType.DMA((rows + len(pieces),)),
        ],
        compiler_params=pltpu.CompilerParams(vmem_limit_bytes=56 << 20),
        name="image_terms",
    )(neighbours, pattern, colour, margin, *pieces)


def per_device(ndomain, ncolour, margin, neighbours, pattern, colour, send_list):
    coeffs = cheb_coefficients()
    rows, _, orbits, _ = margin.shape
    own = neighbours.shape[0]
    pieces = {0: first_terms(ndomain, ncolour, neighbours, pattern, colour, send_list, margin)}
    step = ncolour // 2
    while step:
        pairs = [(i, i ^ step) for i in range(ncolour)]
        for held in list(pieces):
            pieces[held ^ step] = lax.ppermute(pieces[held], "col", pairs)
        step //= 2
    pieces = [pieces[i] for i in range(ncolour)]
    up, down = borders(own, send_list, pieces)
    onward = [(i, (i + 1) % ndomain) for i in range(ndomain)]
    before = lax.ppermute(up, "dom", onward)
    after = lax.ppermute(down, "dom", [(j, i) for i, j in onward])
    images = image_terms(
        coeffs, ncolour, neighbours, pattern, colour, margin, pieces + [before, after]
    )
    images = lax.all_to_all(images, "col", split_axis=0, concat_axis=0, tiled=True)
    return images.reshape(own * orbits, orbits)


def solution(mesh):
    placed = (P(("dom", "col"), None, None, None), P("dom", None), P("dom", None), P(), P())
    return jax.shard_map(
        functools.partial(per_device, mesh.shape["dom"], mesh.shape["col"]),
        mesh=mesh,
        in_specs=placed,
        out_specs=P("dom", "col"),
        check_vma=False,
    )
```

```python
import functools
import math

import jax
import jax.numpy as jnp
from jax import lax
from jax.experimental import pallas as pl
from jax.experimental.pallas import tpu as pltpu
from jax.sharding import PartitionSpec as P

CENTRE = 1.0
HALF_WIDTH = 0.9
HBM = pl.BlockSpec(memory_space=pltpu.HBM)
SMEM = pl.BlockSpec(memory_space=pltpu.SMEM)
VMEM = pl.BlockSpec(memory_space=pltpu.VMEM)
WIRE = jnp.float16
WIRE_SCALE = 0.5


def cheb_coefficients():
    samples = []
    for index_k in range(3):
        angle_value = math.pi * (index_k + 0.5) / 3.0
        samples.append((angle_value, (CENTRE + HALF_WIDTH * math.cos(angle_value)) ** (-0.5)))
    coeffs = []
    for order in range(3):
        coeffs.append(
            2.0
            / 3.0
            * sum((value * math.cos(order * angle_value) for angle_value, value in samples))
        )
    coeffs[0] = 0.5 * coeffs[0]
    return coeffs


def unit(orbits):
    down = lax.broadcasted_iota(jnp.int32, (orbits, orbits), 0)
    along = lax.broadcasted_iota(jnp.int32, (orbits, orbits), 1)
    return (down == along).astype(jnp.float32)


def limit(shapes, extra=2 << 20):
    total = sum(math.prod(s.shape) * jnp.dtype(s.dtype).itemsize for s in shapes)
    return int(total + extra)


def like(shape, dtype):
    return jax.ShapeDtypeStruct(shape, dtype)


def first_kernel(ndomain, ncolour, chunk, *refs):
    tables, margin = refs[:4], refs[4]
    near, far, border, blocks, sums = refs[5:10]
    neighbours, pattern, colour, sends, table, sems, small = refs[10:]
    domain = lax.axis_index("dom")
    shade = lax.axis_index("col")
    rows, slots, orbits, _ = margin.shape
    own = neighbours.shape[0]
    width = sends.shape[1]
    loads = [
        pltpu.make_async_copy(source, target, small.at[i])
        for i, (source, target) in enumerate(zip(tables, (neighbours, pattern, colour, sends)))
    ]
    for load in loads:
        load.start()
    copies = []
    for row in range(rows):
        for i, k in enumerate(range(0, slots, chunk)):
            part = pl.ds(k, min(chunk, slots - k))
            copies.append(
                pltpu.make_async_copy(margin.at[row, part], blocks.at[row, part], sems.at[row, i])
            )
    for copy in copies:
        copy.start()
    sums[...] = jnp.zeros_like(sums)
    border[...] = jnp.zeros_like(border)
    base = shade - lax.rem(shade, 2)
    lower = lax.rem(domain + ndomain - 1, ndomain)
    upper = lax.rem(domain + 1, ndomain)
    for load in loads:
        load.wait()
    for i in range(own):
        table[i] = colour[domain * own + i] ^ base
    for i in range(width):
        table[own + i] = colour[lower * own + sends[1, i, lower]] ^ base
        table[own + width + i] = colour[upper * own + sends[0, i, upper]] ^ base
    eye = unit(orbits)
    half = ncolour // 4
    for row in range(rows):
        block = shade * rows + row
        sums[row, table[block]] = (-CENTRE) * eye
        for k0 in range(0, slots, chunk):
            copies.pop(0).wait()

            @pl.loop(k0, min(k0 + chunk, slots))
            def _(k):
                entry = neighbours[block, k]
                live = pattern[block, k] == 1
                value = blocks[row, k].astype(jnp.float32)
                sums[row, jnp.where(live, table[entry], ncolour)] += value

                @pl.when(jnp.logical_and(live, entry >= own))
                def _():
                    border[row, entry - own] += value

        for c in range(ncolour):
            r = c // 2
            lanes = slice((c % 2) * orbits, (c % 2 + 1) * orbits)
            (near if r < half else far)[r % half, row, :, lanes] = (
                sums[row, c] * (1.0 / HALF_WIDTH)
            ).astype(jnp.bfloat16)


def first_terms(ndomain, ncolour, neighbours, pattern, colour, sends, margin):
    rows, slots, orbits, _ = margin.shape
    width = sends.shape[1]
    ext = neighbours.shape[0] + 2 * width
    half = like((ncolour // 4, rows, orbits, 2 * orbits), jnp.bfloat16)
    border = like((rows, 2 * width, orbits, orbits), jnp.float32)
    sums = like((rows, ncolour + 1, orbits, orbits), jnp.float32)
    chunk = 9
    tables = [neighbours, pattern, colour, sends]
    return pl.pallas_call(
        functools.partial(first_kernel, ndomain, ncolour, chunk),
        out_shape=(half, half, border),
        in_specs=[HBM] * 5,
        out_specs=(VMEM, VMEM, VMEM),
        scratch_shapes=[
            pltpu.VMEM(margin.shape, jnp.bfloat16),
            pltpu.VMEM(sums.shape, jnp.float32),
            *[pltpu.SMEM(t.shape, jnp.int32) for t in tables],
            pltpu.SMEM((ext,), jnp.int32),
            pltpu.SemaphoreType.DMA((rows, pl.cdiv(slots, chunk))),
            pltpu.SemaphoreType.DMA((4,)),
        ],
        compiler_params=pltpu.CompilerParams(
            vmem_limit_bytes=limit([half, half, border, margin, sums])
        ),
        name="first_terms",
    )(*[pltpu.with_memory_space_constraint(t, pltpu.HBM) for t in tables + [margin]])


def border_kernel(sends, near0, far0, near1, far1, up, down):
    domain = lax.axis_index("dom")
    shade = lax.axis_index("col")
    parity = lax.rem(shade, 2)
    half, rows, orbits, _ = near0.shape
    lanes = pl.ds(pl.multiple_of(parity * orbits, orbits), orbits)
    for side, out in ((1, up), (0, down)):
        for i in range(sends.shape[1]):
            entry = sends[side, i, domain]
            relative = lax.div(entry, rows) ^ shade
            row = lax.rem(entry, rows)
            for s in range(2 * half):
                mine, other = (near0, near1) if s < half else (far0, far1)

                @pl.when(relative == 0)
                def _():
                    out[s, i] = mine[s % half, row, :, lanes]

                @pl.when(relative == 1)
                def _():
                    out[s, i] = other[s % half, row, :, lanes]

                @pl.when(relative > 1)
                def _():
                    out[s, i] = jnp.zeros(out.shape[2:], out.dtype)


def borders(sends, near0, far0, near1, far1):
    half, _, orbits, _ = near0.shape
    out = like((2 * half, sends.shape[1], orbits, orbits), jnp.bfloat16)
    return pl.pallas_call(
        border_kernel,
        out_shape=(out, out),
        in_specs=[SMEM] + [VMEM] * 4,
        out_specs=(VMEM, VMEM),
        compiler_params=pltpu.CompilerParams(
            vmem_limit_bytes=limit([near0, far0, near1, far1, out, out])
        ),
        name="borders",
    )(sends, near0, far0, near1, far1)


def image_kernel(coeffs, upper_half, neighbours, pattern, colour, margin, *refs):
    pieces, (images, ext) = refs[:-2], refs[-2:]
    domain = lax.axis_index("dom")
    shade = lax.axis_index("col")
    parity = lax.rem(shade, 2)
    base = shade - parity
    rows, slots, orbits, _ = margin.shape
    own = neighbours.shape[0]
    half = pieces[0].shape[0]
    for r in range(half):
        for relative, piece in enumerate(pieces):
            turn = ((relative // 2) % half) ^ r
            for row in range(rows):
                ext[r, relative * rows + row] = piece[turn, row]
        ext[r, own] = jnp.zeros(ext.shape[2:], ext.dtype)
    eye = unit(orbits)
    for row in range(rows):
        block = shade * rows + row
        mine = colour[domain * own + block] ^ base
        spots = []
        for k in range(slots):
            entry = neighbours[block, k]
            spot = (lax.div(entry, rows) ^ shade) * rows + lax.rem(entry, rows)
            live = jnp.logical_and(pattern[block, k] == 1, entry < own)
            spots.append(jnp.where(live, spot, own))
        for r in range(half):
            total = jnp.zeros((orbits, 2 * orbits), jnp.float32)
            for k in range(0, slots, 2):
                ks = range(k, min(k + 2, slots))
                left = jnp.concatenate([margin[row, j] for j in ks], axis=1)
                right = jnp.concatenate([ext[r, spots[j]] for j in ks], axis=0)
                total += jnp.dot(left, right, preferred_element_type=jnp.float32)
            for q in range(2):
                cut = slice(q * orbits, (q + 1) * orbits)
                first = ext[r, row, :, cut].astype(jnp.float32)
                relative = 2 * (r + (half if upper_half else 0)) + q
                probe = jnp.where(mine == relative, eye, 0.0)
                applied = (total[:, cut] - CENTRE * first) * (1.0 / HALF_WIDTH)
                images[2 * r + (parity ^ q), row] = (
                    coeffs[0] * probe + coeffs[1] * first + coeffs[2] * (2.0 * applied - probe)
                )


def image_terms(coeffs, upper_half, neighbours, pattern, colour, margin, pieces):
    rows, slots, orbits, _ = margin.shape
    half = pieces[0].shape[0]
    images = like((2 * half, rows, orbits, orbits), jnp.float32)
    ext = like((half, neighbours.shape[0] + 1, orbits, 2 * orbits), jnp.bfloat16)
    return pl.pallas_call(
        functools.partial(image_kernel, coeffs, upper_half),
        out_shape=images,
        in_specs=[SMEM] * 3 + [VMEM] * (1 + len(pieces)),
        out_specs=VMEM,
        scratch_shapes=[pltpu.VMEM(ext.shape, ext.dtype)],
        compiler_params=pltpu.CompilerParams(
            vmem_limit_bytes=limit([margin, images, ext, *pieces], 4 << 20)
        ),
        name="image_terms",
    )(neighbours, pattern, colour, margin, *pieces)


def final_kernel(scale, count, mine, *refs):
    images, refs = refs[: count - 1], refs[count - 1 :]
    blocks, refs = refs[:count], refs[count:]
    firsts, out = refs[:-1], refs[-1]
    shade = lax.axis_index("col")
    rows, wide, orbits, _ = blocks[0].shape
    width = wide // 2
    right = []
    for e in range(wide):
        side, i = divmod(e, width)
        value = firsts[side][0, i].astype(jnp.float32)
        for other in firsts[2:]:
            value += other[side, i].astype(jnp.float32)
        right.append(value.astype(jnp.bfloat16))
    right = jnp.concatenate(right + right, axis=0)
    for relative in range(count):
        for row in range(rows):
            left = jnp.concatenate([blocks[relative][row, e] for e in range(wide)], axis=1)
            high = left.astype(jnp.bfloat16)
            low = (left - high.astype(jnp.float32)).astype(jnp.bfloat16)
            extra = jnp.dot(
                jnp.concatenate([high, low], axis=1), right, preferred_element_type=jnp.float32
            )
            if relative == 0:
                value = mine[0, row]
            else:
                value = images[relative - 1][0, row] * (1.0 / WIRE_SCALE)
            at = (shade ^ relative) * rows + row
            out[pl.ds(pl.multiple_of(at * orbits, orbits), orbits), :] = value + scale * extra


def final_images(scale, mine, images, blocks, firsts):
    count = len(blocks)
    rows, _, orbits, _ = blocks[0].shape
    out = like((count * rows * orbits, orbits), jnp.float32)
    return pl.pallas_call(
        functools.partial(final_kernel, scale, count),
        out_shape=out,
        in_specs=[VMEM] * (1 + len(images) + len(blocks) + len(firsts)),
        out_specs=VMEM,
        compiler_params=pltpu.CompilerParams(
            vmem_limit_bytes=limit([mine, *images, *blocks, *firsts, out], 4 << 20)
        ),
        name="final_images",
    )(mine, *images, *blocks, *firsts)


def per_device(ndomain, ncolour, margin, neighbours, pattern, colour, send_list):
    coeffs = cheb_coefficients()
    pairs = ncolour // 2
    half = pairs // 2
    sends = jnp.transpose(send_list, (1, 2, 0))

    def across(value, step):
        return lax.ppermute(value, "col", [(i, i ^ step) for i in range(ncolour)])

    near, far, border = first_terms(ndomain, ncolour, neighbours, pattern, colour, sends, margin)
    nears, fars = {0: near}, {0: far}
    for s in range(1, pairs):
        nears[2 * s] = across(near, 2 * s)
        fars[2 * s] = across(far, 2 * s)
    nears[1] = across(near, 1)
    fars[1] = across(far, 1)
    up, down = borders(sends, near, far, nears[1], fars[1])
    onward = [(i, (i + 1) % ndomain) for i in range(ndomain)]
    before = lax.ppermute(up, "dom", onward)
    after = lax.ppermute(down, "dom", [(j, i) for i, j in onward])
    for s in range(1, pairs):
        nears[2 * s + 1] = across(nears[2 * s], 1)
        fars[2 * s + 1] = across(fars[2 * s], 1)
    wire = border.astype(WIRE)
    wires = {0: wire, 1: across(wire, 1)}
    for s in range(1, pairs):
        wires[2 * s] = across(wire, 2 * s)
        wires[2 * s + 1] = across(wires[2 * s], 1)

    def pieces(upper):
        picked = []
        for relative in range(ncolour):
            top = relative // 2 >= half
            picked.append((nears if top == upper else fars)[relative])
        return picked

    outer = image_terms(coeffs, True, neighbours, pattern, colour, margin, pieces(True))
    images = {}
    sent = (outer * WIRE_SCALE).astype(WIRE)
    for m in range(pairs, ncolour):
        images[m] = across(sent[m - pairs : m - pairs + 1], m)
    firsts = [before, after]
    for s in range(1, pairs):
        firsts.append(across(jnp.stack([before[s], after[s]]), 2 * s))
    inner = image_terms(coeffs, False, neighbours, pattern, colour, margin, pieces(False))
    sent = (inner * WIRE_SCALE).astype(WIRE)
    for m in range(1, pairs):
        images[m] = across(sent[m : m + 1], m)
    return final_images(
        2.0 * coeffs[2] / HALF_WIDTH,
        inner,
        [images[m].astype(jnp.float32) for m in range(1, ncolour)],
        [border] + [wires[m].astype(jnp.float32) for m in range(1, ncolour)],
        firsts,
    )


def solution(mesh):
    placed = (P(("dom", "col"), None, None, None), P("dom", None), P("dom", None), P(), P())
    return jax.shard_map(
        functools.partial(per_device, mesh.shape["dom"], mesh.shape["col"]),
        mesh=mesh,
        in_specs=placed,
        out_specs=P("dom", "col"),
        check_vma=False,
    )
```

```python
import functools
import math

import jax
import jax.numpy as jnp
from jax import lax
from jax.experimental import pallas as pl
from jax.experimental.pallas import tpu as pltpu
from jax.sharding import PartitionSpec as P

CENTRE = 1.0
HALF_WIDTH = 0.9
HBM = pl.BlockSpec(memory_space=pltpu.HBM)
SMEM = pl.BlockSpec(memory_space=pltpu.SMEM)
VMEM = pl.BlockSpec(memory_space=pltpu.VMEM)
WIRE = jnp.float16
WIRE_SCALE = 0.5
CHUNK = 9


def cheb_coefficients():
    samples = []
    for index_k in range(3):
        angle_value = math.pi * (index_k + 0.5) / 3.0
        samples.append((angle_value, (CENTRE + HALF_WIDTH * math.cos(angle_value)) ** (-0.5)))
    coeffs = []
    for order in range(3):
        coeffs.append(
            2.0
            / 3.0
            * sum((value * math.cos(order * angle_value) for angle_value, value in samples))
        )
    coeffs[0] = 0.5 * coeffs[0]
    return coeffs


def unit(orbits):
    down = lax.broadcasted_iota(jnp.int32, (orbits, orbits), 0)
    along = lax.broadcasted_iota(jnp.int32, (orbits, orbits), 1)
    return (down == along).astype(jnp.float32)


def like(shape, dtype):
    return jax.ShapeDtypeStruct(shape, dtype)


def call(kernel, name, ins, outs, scratch, args, extra=2):
    held = [*outs, *(s for s in scratch if isinstance(s, jax.ShapeDtypeStruct))]
    held += [a for spec, a in zip(ins, args) if spec is VMEM]
    total = sum(math.prod(s.shape) * jnp.dtype(s.dtype).itemsize for s in held)
    return pl.pallas_call(
        kernel,
        out_shape=tuple(outs),
        in_specs=ins,
        out_specs=(VMEM,) * len(outs),
        scratch_shapes=[
            pltpu.VMEM(s.shape, s.dtype) if isinstance(s, jax.ShapeDtypeStruct) else s
            for s in scratch
        ],
        compiler_params=pltpu.CompilerParams(vmem_limit_bytes=total + (extra << 20)),
        cost_estimate=pl.CostEstimate(flops=1000, bytes_accessed=1000, transcendentals=0),
        name=name,
    )(*args)


def first_kernel(ndomain, ncolour, *refs):
    tables, margin = refs[:4], refs[4]
    near, far, sums, blocks, totals = refs[5:10]
    neighbours, pattern, colour, sends, table, sems, small = refs[10:]
    domain = lax.axis_index("dom")
    shade = lax.axis_index("col")
    rows, slots, orbits, _ = margin.shape
    own = neighbours.shape[0]
    width = sends.shape[1]
    loads = [
        pltpu.make_async_copy(source, target, small.at[i])
        for i, (source, target) in enumerate(zip(tables, (neighbours, pattern, colour, sends)))
    ]
    for load in loads:
        load.start()
    copies = []
    for row in range(rows):
        for i, k in enumerate(range(0, slots, CHUNK)):
            part = pl.ds(k, min(CHUNK, slots - k))
            copies.append(
                pltpu.make_async_copy(margin.at[row, part], blocks.at[row, part], sems.at[row, i])
            )
    for copy in copies:
        copy.start()
    sums[...] = jnp.zeros_like(sums)
    totals[...] = jnp.zeros_like(totals)
    base = shade - lax.rem(shade, 2)
    lower = lax.rem(domain + ndomain - 1, ndomain)
    upper = lax.rem(domain + 1, ndomain)
    for load in loads:
        load.wait()
    for i in range(own):
        table[i] = colour[domain * own + i] ^ base
    for i in range(width):
        table[own + i] = colour[lower * own + sends[1, i, lower]] ^ base
        table[own + width + i] = colour[upper * own + sends[0, i, upper]] ^ base
    eye = unit(orbits)
    half = ncolour // 4
    for row in range(rows):
        block = shade * rows + row
        totals[row, table[block]] = (-CENTRE) * eye
        for k0 in range(0, slots, CHUNK):
            copies.pop(0).wait()

            @pl.loop(k0, min(k0 + CHUNK, slots))
            def _(k):
                entry = jnp.where(pattern[block, k] == 1, neighbours[block, k], own + 2 * width)
                sums[row, entry] += blocks[row, k].astype(jnp.float32)

        @pl.loop(0, own + 2 * width)
        def _(entry):
            totals[row, table[entry]] += sums[row, entry]

        for c in range(ncolour):
            r = c // 2
            (near if r < half else far)[r % half, c % 2, row] = (
                totals[row, c] * (1.0 / HALF_WIDTH)
            ).astype(jnp.bfloat16)


def first_terms(ndomain, ncolour, neighbours, pattern, colour, sends, margin):
    rows, slots, orbits, _ = margin.shape
    ext = neighbours.shape[0] + 2 * sends.shape[1]
    half = like((ncolour // 4, 2, rows, orbits, orbits), jnp.bfloat16)
    sums = like((rows, ext + 1, orbits, orbits), jnp.float32)
    tables = [neighbours, pattern, colour, sends]
    return call(
        functools.partial(first_kernel, ndomain, ncolour),
        "first_terms",
        [HBM] * 5,
        [half, half, sums],
        [
            like(margin.shape, margin.dtype),
            like((rows, ncolour, orbits, orbits), jnp.float32),
            *[pltpu.SMEM(t.shape, jnp.int32) for t in tables],
            pltpu.SMEM((ext,), jnp.int32),
            pltpu.SemaphoreType.DMA((rows, pl.cdiv(slots, CHUNK))),
            pltpu.SemaphoreType.DMA((4,)),
        ],
        [pltpu.with_memory_space_constraint(t, pltpu.HBM) for t in tables + [margin]],
    )


def border_kernel(sends, near0, far0, near1, far1, up, down):
    domain = lax.axis_index("dom")
    shade = lax.axis_index("col")
    parity = lax.rem(shade, 2)
    half, _, rows, orbits, _ = near0.shape
    for side, out in ((1, up), (0, down)):
        for i in range(sends.shape[1]):
            entry = sends[side, i, domain]
            relative = lax.div(entry, rows) ^ shade
            row = lax.rem(entry, rows)

            @pl.when(relative == 0)
            def _():
                for s in range(2 * half):
                    out[s, i] = (near0 if s < half else far0)[s % half, parity, row]

            @pl.when(relative == 1)
            def _():
                for s in range(2 * half):
                    out[s, i] = (near1 if s < half else far1)[s % half, parity, row]

            @pl.when(relative > 1)
            def _():
                for s in range(2 * half):
                    out[s, i] = jnp.zeros(out.shape[2:], out.dtype)


def borders(sends, near0, far0, near1, far1):
    half, _, _, orbits, _ = near0.shape
    out = like((2 * half, sends.shape[1], orbits, orbits), jnp.bfloat16)
    return call(
        border_kernel,
        "borders",
        [SMEM] + [VMEM] * 4,
        [out, out],
        [],
        [sends, near0, far0, near1, far1],
    )


def split_kernel(own, sums, left):
    shade = lax.axis_index("col")
    rows, _, orbits, _ = sums.shape
    for spot in range(own):
        entry = ((spot // rows) ^ shade) * rows + spot % rows
        for row in range(rows):
            value = sums[row, entry]
            high = value.astype(jnp.bfloat16)
            low = (value - high.astype(jnp.float32)).astype(jnp.bfloat16)
            lanes = slice(spot * orbits, (spot + 1) * orbits)
            left[2 * row * orbits : (2 * row + 1) * orbits, lanes] = high
            left[(2 * row + 1) * orbits : (2 * row + 2) * orbits, lanes] = low


def split_sums(own, sums):
    rows, _, orbits, _ = sums.shape
    left = like((2 * rows * orbits, own * orbits), jnp.bfloat16)
    return call(functools.partial(split_kernel, own), "split_sums", [VMEM], [left], [], [sums])[0]


def image_kernel(coeffs, upper_half, own, colour, left, *refs):
    pieces, images = refs[:-1], refs[-1]
    domain = lax.axis_index("dom")
    shade = lax.axis_index("col")
    parity = lax.rem(shade, 2)
    base = shade - parity
    half, _, rows, orbits, _ = pieces[0].shape
    eye = unit(orbits)
    for r in range(half):
        right = []
        for relative, piece in enumerate(pieces):
            turn = ((relative // 2) % half) ^ r
            for row in range(rows):
                right.append(jnp.concatenate([piece[turn, 0, row], piece[turn, 1, row]], axis=1))
        total = jnp.dot(
            left[...], jnp.concatenate(right, axis=0), preferred_element_type=jnp.float32
        )
        for row in range(rows):
            mine = colour[domain * own + shade * rows + row] ^ base
            high = total[2 * row * orbits : (2 * row + 1) * orbits]
            low = total[(2 * row + 1) * orbits : (2 * row + 2) * orbits]
            product = high + low
            for q in range(2):
                first = pieces[0][r, q, row].astype(jnp.float32)
                relative = 2 * (r + (half if upper_half else 0)) + q
                probe = jnp.where(mine == relative, eye, 0.0)
                applied = product[:, q * orbits : (q + 1) * orbits] - CENTRE * first
                applied = applied * (1.0 / HALF_WIDTH)
                images[2 * r + (parity ^ q), row] = (
                    coeffs[0] * probe + coeffs[1] * first + coeffs[2] * (2.0 * applied - probe)
                )


def image_terms(coeffs, upper_half, own, colour, left, pieces):
    half, _, rows, orbits, _ = pieces[0].shape
    images = like((2 * half, rows, orbits, orbits), jnp.float32)
    return call(
        functools.partial(image_kernel, coeffs, upper_half, own),
        "image_terms",
        [SMEM] + [VMEM] * (1 + len(pieces)),
        [images],
        [],
        [colour, left, *pieces],
        4,
    )[0]


def final_kernel(scale, count, mine, *refs):
    images, refs = refs[: count - 1], refs[count - 1 :]
    blocks, refs = refs[:count], refs[count:]
    firsts, out = refs[:-1], refs[-1]
    shade = lax.axis_index("col")
    rows, wide, orbits, _ = blocks[0].shape
    width = wide // 2
    right = []
    for e in range(wide):
        side, i = divmod(e, width)
        value = firsts[side][0, i].astype(jnp.float32)
        for other in firsts[2:]:
            value += other[side, i].astype(jnp.float32)
        right.append(value.astype(jnp.bfloat16))
    right = jnp.concatenate(right + right, axis=0)
    for relative in range(count):
        for row in range(rows):
            left = jnp.concatenate([blocks[relative][row, e] for e in range(wide)], axis=1)
            high = left.astype(jnp.bfloat16)
            low = (left - high.astype(jnp.float32)).astype(jnp.bfloat16)
            extra = jnp.dot(
                jnp.concatenate([high, low], axis=1), right, preferred_element_type=jnp.float32
            )
            if relative == 0:
                value = mine[0, row]
            else:
                value = images[relative - 1][row] * (1.0 / WIRE_SCALE)
            at = (shade ^ relative) * rows + row
            out[pl.ds(pl.multiple_of(at * orbits, orbits), orbits), :] = value + scale * extra


def final_images(scale, mine, images, blocks, firsts):
    count = len(blocks)
    rows, _, orbits, _ = blocks[0].shape
    return call(
        functools.partial(final_kernel, scale, count),
        "final_images",
        [VMEM] * (1 + len(images) + len(blocks) + len(firsts)),
        [like((count * rows * orbits, orbits), jnp.float32)],
        [],
        [mine, *images, *blocks, *firsts],
        4,
    )[0]


def per_device(ndomain, ncolour, margin, neighbours, pattern, colour, send_list):
    coeffs = cheb_coefficients()
    pairs = ncolour // 2
    half = pairs // 2
    sends = jnp.transpose(send_list, (1, 2, 0))
    rows, width = margin.shape[0], send_list.shape[2]
    own = neighbours.shape[0]

    def across(value, step):
        return lax.ppermute(value, "col", [(i, i ^ step) for i in range(ncolour)])

    near, far, sums = first_terms(ndomain, ncolour, neighbours, pattern, colour, sends, margin)
    border = sums[:, own : own + 2 * width]
    left = split_sums(own, sums)
    wire = border.astype(WIRE)
    nears, fars, wires = {0: near}, {0: far}, [wire]
    for s in range(1, pairs):
        nears[2 * s] = across(near, 2 * s)
        fars[2 * s] = across(far, 2 * s)
    nears[1] = across(near, 1)
    fars[1] = across(far, 1)
    up, down = borders(sends, near, far, nears[1], fars[1])
    onward = [(i, (i + 1) % ndomain) for i in range(ndomain)]
    before = lax.ppermute(up, "dom", onward)
    after = lax.ppermute(down, "dom", [(j, i) for i, j in onward])
    for s in range(1, pairs):
        wires.append(across(wire, 2 * s))
    for s in range(1, pairs):
        nears[2 * s], _, _ = lax.optimization_barrier((nears[2 * s], up, down))
        nears[2 * s + 1] = across(nears[2 * s], 1)
    for s in range(1, pairs):
        fars[2 * s + 1] = across(fars[2 * s], 1)

    def pieces(upper):
        picked = []
        for relative in range(ncolour):
            top = relative // 2 >= half
            picked.append((nears if top == upper else fars)[relative])
        return picked

    outer = image_terms(coeffs, True, own, colour, left, pieces(True))
    before, after, outer = lax.optimization_barrier((before, after, outer))
    others = across(jnp.concatenate(wires), 1)
    blocks = []
    for s in range(pairs):
        for side in (wires[s], others[s * rows : (s + 1) * rows]):
            blocks.append(side.astype(jnp.float32))
    blocks[0] = border
    images = {}
    sent = (outer * WIRE_SCALE).astype(WIRE)
    for m in range(pairs, ncolour):
        images[m] = sent[m - pairs]
    inner = image_terms(coeffs, False, own, colour, left, pieces(False))
    sent = (inner * WIRE_SCALE).astype(WIRE)
    for m in range(1, pairs):
        images[m] = sent[m]
    firsts = [before, after]
    for m in images:
        if m % 2:
            images[m] = across(images[m], m)
        else:
            second = jnp.stack([before[m // 2], after[m // 2]]).astype(WIRE)
            sent = jnp.concatenate([images[m], second.reshape((-1,) + images[m].shape[1:])])
            sent = across(sent, m)
            images[m], second = sent[:rows], sent[rows:]
            firsts.append(second.reshape((2, width) + second.shape[1:]).astype(jnp.bfloat16))
    return final_images(
        2.0 * coeffs[2] / HALF_WIDTH,
        inner,
        [images[m].astype(jnp.float32) for m in range(1, ncolour)],
        blocks,
        firsts,
    )


def solution(mesh):
    placed = (P(("dom", "col"), None, None, None), P("dom", None), P("dom", None), P(), P())
    return jax.shard_map(
        functools.partial(per_device, mesh.shape["dom"], mesh.shape["col"]),
        mesh=mesh,
        in_specs=placed,
        out_specs=P("dom", "col"),
        check_vma=False,
    )
```

```python
import functools
import math

import jax
import jax.numpy as jnp
from jax import lax
from jax.experimental import pallas as pl
from jax.experimental.pallas import tpu as pltpu
from jax.sharding import PartitionSpec as P

CENTRE = 1.0
HALF_WIDTH = 0.9
HBM = pl.BlockSpec(memory_space=pltpu.HBM)
SMEM = pl.BlockSpec(memory_space=pltpu.SMEM)
VMEM = pl.BlockSpec(memory_space=pltpu.VMEM)
WIRE = jnp.float16
WIRE_SCALE = 0.5
CHUNK = 9


def cheb_coefficients():
    samples = []
    for index_k in range(3):
        angle_value = math.pi * (index_k + 0.5) / 3.0
        samples.append((angle_value, (CENTRE + HALF_WIDTH * math.cos(angle_value)) ** (-0.5)))
    coeffs = []
    for order in range(3):
        coeffs.append(
            2.0
            / 3.0
            * sum((value * math.cos(order * angle_value) for angle_value, value in samples))
        )
    coeffs[0] = 0.5 * coeffs[0]
    return coeffs


def unit(orbits):
    down = lax.broadcasted_iota(jnp.int32, (orbits, orbits), 0)
    along = lax.broadcasted_iota(jnp.int32, (orbits, orbits), 1)
    return (down == along).astype(jnp.float32)


def like(shape, dtype):
    return jax.ShapeDtypeStruct(shape, dtype)


def call(kernel, name, ins, outs, scratch, args, extra=2, cost=1000, out_space=VMEM):
    held = [*outs, *(s for s in scratch if isinstance(s, jax.ShapeDtypeStruct))]
    held += [a for spec, a in zip(ins, args) if spec is VMEM]
    total = sum(math.prod(s.shape) * jnp.dtype(s.dtype).itemsize for s in held)
    return pl.pallas_call(
        kernel,
        out_shape=tuple(outs),
        in_specs=ins,
        out_specs=(out_space,) * len(outs),
        scratch_shapes=[
            pltpu.VMEM(s.shape, s.dtype) if isinstance(s, jax.ShapeDtypeStruct) else s
            for s in scratch
        ],
        compiler_params=pltpu.CompilerParams(vmem_limit_bytes=total + (extra << 20)),
        cost_estimate=pl.CostEstimate(flops=cost, bytes_accessed=1000, transcendentals=0),
        name=name,
    )(*args)


def first_kernel(ndomain, ncolour, *refs):
    tables, margin = refs[:4], refs[4]
    near, far, sums, blocks, totals = refs[5:10]
    neighbours, pattern, colour, sends, table, sems, small = refs[10:]
    domain = lax.axis_index("dom")
    shade = lax.axis_index("col")
    rows, slots, orbits, _ = margin.shape
    own = neighbours.shape[0]
    width = sends.shape[1]
    loads = [
        pltpu.make_async_copy(source, target, small.at[i])
        for i, (source, target) in enumerate(zip(tables, (neighbours, pattern, colour, sends)))
    ]
    for load in loads:
        load.start()
    copies = []
    for row in range(rows):
        for i, k in enumerate(range(0, slots, CHUNK)):
            part = pl.ds(k, min(CHUNK, slots - k))
            copies.append(
                pltpu.make_async_copy(margin.at[row, part], blocks.at[row, part], sems.at[row, i])
            )
    for copy in copies:
        copy.start()
    sums[...] = jnp.zeros_like(sums)
    totals[...] = jnp.zeros_like(totals)
    base = shade - lax.rem(shade, 2)
    lower = lax.rem(domain + ndomain - 1, ndomain)
    upper = lax.rem(domain + 1, ndomain)
    for load in loads:
        load.wait()
    for i in range(own):
        table[i] = colour[domain * own + i] ^ base
    for i in range(width):
        table[own + i] = colour[lower * own + sends[1, i, lower]] ^ base
        table[own + width + i] = colour[upper * own + sends[0, i, upper]] ^ base
    eye = unit(orbits)
    half = ncolour // 4
    for row in range(rows):
        block = shade * rows + row
        totals[row, table[block]] = (-CENTRE) * eye
        for k0 in range(0, slots, CHUNK):
            copies.pop(0).wait()

            @pl.loop(k0, min(k0 + CHUNK, slots), unroll=9)
            def _(k):
                entry = jnp.where(pattern[block, k] == 1, neighbours[block, k], own + 2 * width)
                sums[row, entry] += blocks[row, k].astype(jnp.float32)

        @pl.loop(0, own + 2 * width)
        def _(entry):
            totals[row, table[entry]] += sums[row, entry]

        for c in range(ncolour):
            r = c // 2
            (near if r < half else far)[r % half, c % 2, row] = (
                totals[row, c] * (1.0 / HALF_WIDTH)
            ).astype(jnp.bfloat16)


def first_terms(ndomain, ncolour, neighbours, pattern, colour, sends, margin):
    rows, slots, orbits, _ = margin.shape
    ext = neighbours.shape[0] + 2 * sends.shape[1]
    half = like((ncolour // 4, 2, rows, orbits, orbits), jnp.bfloat16)
    sums = like((rows, ext + 1, orbits, orbits), jnp.float32)
    tables = [neighbours, pattern, colour, sends]
    return call(
        functools.partial(first_kernel, ndomain, ncolour),
        "first_terms",
        [HBM] * 5,
        [half, half, sums],
        [
            like(margin.shape, margin.dtype),
            like((rows, ncolour, orbits, orbits), jnp.float32),
            *[pltpu.SMEM(t.shape, jnp.int32) for t in tables],
            pltpu.SMEM((ext,), jnp.int32),
            pltpu.SemaphoreType.DMA((rows, pl.cdiv(slots, CHUNK))),
            pltpu.SemaphoreType.DMA((4,)),
        ],
        [pltpu.with_memory_space_constraint(t, pltpu.HBM) for t in tables + [margin]],
    )


def border_kernel(sends, near0, far0, near1, far1, up, down):
    domain = lax.axis_index("dom")
    shade = lax.axis_index("col")
    parity = lax.rem(shade, 2)
    half, _, rows, orbits, _ = near0.shape
    for side, out in ((1, up), (0, down)):
        for i in range(sends.shape[1]):
            entry = sends[side, i, domain]
            relative = lax.div(entry, rows) ^ shade
            row = lax.rem(entry, rows)

            @pl.when(relative == 0)
            def _():
                for s in range(2 * half):
                    out[s, i] = (near0 if s < half else far0)[s % half, parity, row]

            @pl.when(relative == 1)
            def _():
                for s in range(2 * half):
                    out[s, i] = (near1 if s < half else far1)[s % half, parity, row]

            @pl.when(relative > 1)
            def _():
                for s in range(2 * half):
                    out[s, i] = jnp.zeros(out.shape[2:], out.dtype)


def borders(sends, near0, far0, near1, far1):
    half, _, _, orbits, _ = near0.shape
    out = like((2 * half, sends.shape[1], orbits, orbits), jnp.bfloat16)
    return call(
        border_kernel,
        "borders",
        [SMEM] + [VMEM] * 4,
        [out, out],
        [],
        [sends, near0, far0, near1, far1],
        cost=1000,
    )


def split_kernel(own, sums, left):
    shade = lax.axis_index("col")
    rows, _, orbits, _ = sums.shape
    for spot in range(own):
        entry = ((spot // rows) ^ shade) * rows + spot % rows
        for row in range(rows):
            value = sums[row, entry]
            high = value.astype(jnp.bfloat16)
            low = (value - high.astype(jnp.float32)).astype(jnp.bfloat16)
            lanes = slice(spot * orbits, (spot + 1) * orbits)
            left[2 * row * orbits : (2 * row + 1) * orbits, lanes] = high
            left[(2 * row + 1) * orbits : (2 * row + 2) * orbits, lanes] = low


def split_sums(own, sums):
    rows, _, orbits, _ = sums.shape
    left = like((2 * rows * orbits, own * orbits), jnp.bfloat16)
    return call(
        functools.partial(split_kernel, own), "split_sums", [VMEM], [left], [], [sums], cost=1000
    )[0]


def image_kernel(coeffs, upper_half, own, colour, left, *refs):
    pieces, images = refs[:-1], refs[-1]
    domain = lax.axis_index("dom")
    shade = lax.axis_index("col")
    parity = lax.rem(shade, 2)
    base = shade - parity
    half, _, rows, orbits, _ = pieces[0].shape
    eye = unit(orbits)
    for r in range(half):
        right = []
        for relative, piece in enumerate(pieces):
            turn = ((relative // 2) % half) ^ r
            for row in range(rows):
                right.append(jnp.concatenate([piece[turn, 0, row], piece[turn, 1, row]], axis=1))
        total = jnp.dot(
            left[...], jnp.concatenate(right, axis=0), preferred_element_type=jnp.float32
        )
        for row in range(rows):
            mine = colour[domain * own + shade * rows + row] ^ base
            high = total[2 * row * orbits : (2 * row + 1) * orbits]
            low = total[(2 * row + 1) * orbits : (2 * row + 2) * orbits]
            product = high + low
            for q in range(2):
                first = pieces[0][r, q, row].astype(jnp.float32)
                relative = 2 * (r + (half if upper_half else 0)) + q
                probe = jnp.where(mine == relative, eye, 0.0)
                applied = product[:, q * orbits : (q + 1) * orbits] - CENTRE * first
                applied = applied * (1.0 / HALF_WIDTH)
                images[2 * r + (parity ^ q), row] = (
                    coeffs[0] * probe + coeffs[1] * first + coeffs[2] * (2.0 * applied - probe)
                )


def image_terms(coeffs, upper_half, own, colour, left, pieces):
    half, _, rows, orbits, _ = pieces[0].shape
    images = like((2 * half, rows, orbits, orbits), jnp.float32)
    return call(
        functools.partial(image_kernel, coeffs, upper_half, own),
        "image_terms",
        [SMEM] + [VMEM] * (1 + len(pieces)),
        [images],
        [],
        [colour, left, *pieces],
        4,
        1000,
    )[0]


def final_kernel(scale, count, mine, *refs):
    images, refs = refs[: count - 1], refs[count - 1 :]
    blocks, refs = refs[:count], refs[count:]
    firsts, (out, value, sems) = refs[:-3], refs[-3:]
    shade = lax.axis_index("col")
    rows, wide, orbits, _ = blocks[0].shape
    width = wide // 2
    right = []
    for e in range(wide):
        side, i = divmod(e, width)
        first = firsts[side][0, i].astype(jnp.float32)
        for other in firsts[2:]:
            first += other[1 - side, i].astype(jnp.float32)
        right.append(first.astype(jnp.bfloat16))
    right = jnp.concatenate(right + right, axis=0)
    copies = []
    for relative in range(count):
        left = [
            jnp.concatenate([blocks[relative][row, e] for row in range(rows)], axis=0)
            for e in range(wide)
        ]
        left = jnp.concatenate(left, axis=1)
        high = left.astype(jnp.bfloat16)
        low = (left - high.astype(jnp.float32)).astype(jnp.bfloat16)
        extra = jnp.dot(
            jnp.concatenate([high, low], axis=1), right, preferred_element_type=jnp.float32
        )
        if relative == 0:
            image = mine[0]
        else:
            image = images[relative - 1][...] * (1.0 / WIRE_SCALE)
        value[relative] = image.reshape(rows * orbits, orbits) + scale * extra
        at = pl.multiple_of((shade ^ relative) * (rows * orbits), rows * orbits)
        copy = pltpu.make_async_copy(
            value.at[relative], out.at[pl.ds(at, rows * orbits)], sems.at[relative]
        )
        copy.start()
        copies.append(copy)
    for copy in copies:
        copy.wait()


def final_images(scale, mine, images, blocks, firsts):
    count = len(blocks)
    rows, _, orbits, _ = blocks[0].shape
    size = rows * orbits
    return call(
        functools.partial(final_kernel, scale, count),
        "final_images",
        [VMEM] * (1 + len(images) + len(blocks) + len(firsts)),
        [like((count * size, orbits), jnp.float32)],
        [like((count, size, orbits), jnp.float32), pltpu.SemaphoreType.DMA((count,))],
        [mine, *images, *blocks, *firsts],
        4,
        out_space=HBM,
    )[0]


def per_device(ndomain, ncolour, margin, neighbours, pattern, colour, send_list):
    coeffs = cheb_coefficients()
    pairs = ncolour // 2
    half = pairs // 2
    sends = jnp.transpose(send_list, (1, 2, 0))
    rows, width = margin.shape[0], send_list.shape[2]
    own = neighbours.shape[0]

    def across(value, step):
        return lax.ppermute(value, "col", [(i, i ^ step) for i in range(ncolour)])

    near, far, sums = first_terms(ndomain, ncolour, neighbours, pattern, colour, sends, margin)
    border = sums[:, own : own + 2 * width]
    wire = border.astype(WIRE)
    nears, fars, wires = {0: near}, {0: far}, {0: wire}
    nears[1] = across(near, 1)
    fars[1] = across(far, 1)
    near_out, far_out = near, far
    for s in range(1, pairs):
        nears[2 * s] = across(near_out, 2 * s)
        fars[2 * s] = across(far_out, 2 * s)
    up, down = borders(sends, near, far, nears[1], fars[1])
    onward = [(i, (i + 1) % ndomain) for i in range(ndomain)]
    before = lax.ppermute(up, "dom", onward)
    after = lax.ppermute(down, "dom", [(j, i) for i, j in onward])
    for s in range(1, pairs):
        wires[2 * s] = across(wire, 2 * s)
    left = split_sums(own, sums)
    for s in range(1, pairs):
        nears[2 * s], _, _ = lax.optimization_barrier((nears[2 * s], up, down))
        nears[2 * s + 1] = across(nears[2 * s], 1)
    for s in range(1, pairs):
        fars[2 * s + 1] = across(fars[2 * s], 1)

    def pieces(upper):
        picked = []
        for relative in range(ncolour):
            top = relative // 2 >= half
            picked.append((nears if top == upper else fars)[relative])
        return picked

    outer = image_terms(coeffs, True, own, colour, left, pieces(True))
    before, after, outer = lax.optimization_barrier((before, after, outer))
    others = across(jnp.concatenate([wires[2 * s] for s in range(pairs)]), 1)
    for s in range(pairs):
        wires[2 * s + 1] = others[s * rows : (s + 1) * rows]
    blocks = [border] + [wires[m].astype(jnp.float32) for m in range(1, ncolour)]
    images = {}
    sent = (outer * WIRE_SCALE).astype(WIRE)
    for m in range(pairs, ncolour):
        images[m] = sent[m - pairs]
    inner = image_terms(coeffs, False, own, colour, left, pieces(False))
    sent = (inner * WIRE_SCALE).astype(WIRE)
    for m in range(1, pairs):
        images[m] = sent[m]
    firsts = [before, after]
    for m in images:
        if m % 2:
            images[m] = across(images[m], m)
        else:
            second = jnp.stack([after[m // 2], before[m // 2]]).astype(WIRE)
            sent = jnp.concatenate([images[m], second.reshape((-1,) + images[m].shape[1:])])
            sent = across(sent, m)
            images[m], second = sent[:rows], sent[rows:]
            firsts.append(second.reshape((2, width) + second.shape[1:]).astype(jnp.bfloat16))
    return final_images(
        2.0 * coeffs[2] / HALF_WIDTH,
        inner,
        [images[m].astype(jnp.float32) for m in range(1, ncolour)],
        blocks,
        firsts,
    )


def solution(mesh):
    placed = (P(("dom", "col"), None, None, None), P("dom", None), P("dom", None), P(), P())
    return jax.shard_map(
        functools.partial(per_device, mesh.shape["dom"], mesh.shape["col"]),
        mesh=mesh,
        in_specs=placed,
        out_specs=P("dom", "col"),
        check_vma=False,
    )
```

```python
import functools
import math

import jax
import jax.numpy as jnp
from jax import lax
from jax.experimental import pallas as pl
from jax.experimental.pallas import tpu as pltpu
from jax.sharding import PartitionSpec as P

CENTRE = 1.0
HALF_WIDTH = 0.9
HBM = pl.BlockSpec(memory_space=pltpu.HBM)
SMEM = pl.BlockSpec(memory_space=pltpu.SMEM)
VMEM = pl.BlockSpec(memory_space=pltpu.VMEM)
WIRE = jnp.float16
WIRE_SCALE = 0.5
CHUNK = 9


def cheb_coefficients():
    samples = []
    for index_k in range(3):
        angle_value = math.pi * (index_k + 0.5) / 3.0
        samples.append((angle_value, (CENTRE + HALF_WIDTH * math.cos(angle_value)) ** (-0.5)))
    coeffs = []
    for order in range(3):
        coeffs.append(
            2.0
            / 3.0
            * sum((value * math.cos(order * angle_value) for angle_value, value in samples))
        )
    coeffs[0] = 0.5 * coeffs[0]
    return coeffs


def unit(orbits):
    down = lax.broadcasted_iota(jnp.int32, (orbits, orbits), 0)
    along = lax.broadcasted_iota(jnp.int32, (orbits, orbits), 1)
    return (down == along).astype(jnp.float32)


def like(shape, dtype):
    return jax.ShapeDtypeStruct(shape, dtype)


def call(kernel, name, ins, outs, scratch, args, extra=2, cost=1000, out_space=VMEM):
    held = [*outs, *(s for s in scratch if isinstance(s, jax.ShapeDtypeStruct))]
    held += [a for spec, a in zip(ins, args) if spec is VMEM]
    total = sum(math.prod(s.shape) * jnp.dtype(s.dtype).itemsize for s in held)
    return pl.pallas_call(
        kernel,
        out_shape=tuple(outs),
        in_specs=ins,
        out_specs=(out_space,) * len(outs),
        scratch_shapes=[
            pltpu.VMEM(s.shape, s.dtype) if isinstance(s, jax.ShapeDtypeStruct) else s
            for s in scratch
        ],
        compiler_params=pltpu.CompilerParams(vmem_limit_bytes=total + (extra << 20)),
        cost_estimate=pl.CostEstimate(flops=cost, bytes_accessed=1000, transcendentals=0),
        name=name,
    )(*args)


def first_kernel(ndomain, ncolour, *refs):
    tables, margin = refs[:4], refs[4]
    near, far, sums, blocks, totals = refs[5:10]
    neighbours, pattern, colour, sends, table, sems, small = refs[10:]
    domain = lax.axis_index("dom")
    shade = lax.axis_index("col")
    rows, slots, orbits, _ = margin.shape
    own = neighbours.shape[0]
    width = sends.shape[1]
    loads = [
        pltpu.make_async_copy(source, target, small.at[i])
        for i, (source, target) in enumerate(zip(tables, (neighbours, pattern, colour, sends)))
    ]
    for load in loads:
        load.start()
    copies = []
    for row in range(rows):
        for i, k in enumerate(range(0, slots, CHUNK)):
            part = pl.ds(k, min(CHUNK, slots - k))
            copies.append(
                pltpu.make_async_copy(margin.at[row, part], blocks.at[row, part], sems.at[row, i])
            )
    for copy in copies:
        copy.start()
    sums[...] = jnp.zeros_like(sums)
    totals[...] = jnp.zeros_like(totals)
    base = shade - lax.rem(shade, 2)
    lower = lax.rem(domain + ndomain - 1, ndomain)
    upper = lax.rem(domain + 1, ndomain)
    for load in loads:
        load.wait()
    for i in range(own):
        table[i] = colour[domain * own + i] ^ base
    for i in range(width):
        table[own + i] = colour[lower * own + sends[1, i, lower]] ^ base
        table[own + width + i] = colour[upper * own + sends[0, i, upper]] ^ base
    eye = unit(orbits)
    half = ncolour // 4
    for row in range(rows):
        block = shade * rows + row
        totals[row, table[block]] = (-CENTRE) * eye
        for k0 in range(0, slots, CHUNK):
            copies.pop(0).wait()

            @pl.loop(k0, min(k0 + CHUNK, slots), unroll=9)
            def _(k):
                entry = jnp.where(pattern[block, k] == 1, neighbours[block, k], own + 2 * width)
                sums[row, entry] += blocks[row, k].astype(jnp.float32)

        @pl.loop(0, own + 2 * width, unroll=5)
        def _(entry):
            totals[row, table[entry]] += sums[row, entry]

        for c in range(ncolour):
            r = c // 2
            (near if r < half else far)[r % half, c % 2, row] = (
                totals[row, c] * (1.0 / HALF_WIDTH)
            ).astype(jnp.bfloat16)


def first_terms(ndomain, ncolour, neighbours, pattern, colour, sends, margin):
    rows, slots, orbits, _ = margin.shape
    ext = neighbours.shape[0] + 2 * sends.shape[1]
    half = like((ncolour // 4, 2, rows, orbits, orbits), jnp.bfloat16)
    sums = like((rows, ext + 1, orbits, orbits), jnp.float32)
    tables = [neighbours, pattern, colour, sends]
    return call(
        functools.partial(first_kernel, ndomain, ncolour),
        "first_terms",
        [HBM] * 5,
        [half, half, sums],
        [
            like(margin.shape, margin.dtype),
            like((rows, ncolour, orbits, orbits), jnp.float32),
            *[pltpu.SMEM(t.shape, jnp.int32) for t in tables],
            pltpu.SMEM((ext,), jnp.int32),
            pltpu.SemaphoreType.DMA((rows, pl.cdiv(slots, CHUNK))),
            pltpu.SemaphoreType.DMA((4,)),
        ],
        [pltpu.with_memory_space_constraint(t, pltpu.HBM) for t in tables + [margin]],
    )


def border_kernel(sends, near0, far0, near1, far1, up, down):
    domain = lax.axis_index("dom")
    shade = lax.axis_index("col")
    parity = lax.rem(shade, 2)
    half, _, rows, orbits, _ = near0.shape
    for side, out in ((1, up), (0, down)):
        for i in range(sends.shape[1]):
            entry = sends[side, i, domain]
            relative = lax.div(entry, rows) ^ shade
            row = lax.rem(entry, rows)

            @pl.when(relative == 0)
            def _():
                for s in range(2 * half):
                    out[s, i] = (near0 if s < half else far0)[s % half, parity, row]

            @pl.when(relative == 1)
            def _():
                for s in range(2 * half):
                    out[s, i] = (near1 if s < half else far1)[s % half, parity, row]

            @pl.when(relative > 1)
            def _():
                for s in range(2 * half):
                    out[s, i] = jnp.zeros(out.shape[2:], out.dtype)


def borders(sends, near0, far0, near1, far1):
    half, _, _, orbits, _ = near0.shape
    out = like((2 * half, sends.shape[1], orbits, orbits), jnp.bfloat16)
    return call(
        border_kernel,
        "borders",
        [SMEM] + [VMEM] * 4,
        [out, out],
        [],
        [sends, near0, far0, near1, far1],
        cost=1000,
    )


def split_kernel(own, sums, left):
    shade = lax.axis_index("col")
    rows, _, orbits, _ = sums.shape
    for spot in range(own):
        entry = ((spot // rows) ^ shade) * rows + spot % rows
        for row in range(rows):
            value = sums[row, entry]
            high = value.astype(jnp.bfloat16)
            low = (value - high.astype(jnp.float32)).astype(jnp.bfloat16)
            lanes = slice(spot * orbits, (spot + 1) * orbits)
            left[2 * row * orbits : (2 * row + 1) * orbits, lanes] = high
            left[(2 * row + 1) * orbits : (2 * row + 2) * orbits, lanes] = low


def split_sums(own, sums):
    rows, _, orbits, _ = sums.shape
    left = like((2 * rows * orbits, own * orbits), jnp.bfloat16)
    return call(
        functools.partial(split_kernel, own), "split_sums", [VMEM], [left], [], [sums], cost=1000
    )[0]


def image_kernel(coeffs, upper_half, own, colour, left, *refs):
    pieces, images = refs[:-1], refs[-1]
    domain = lax.axis_index("dom")
    shade = lax.axis_index("col")
    parity = lax.rem(shade, 2)
    base = shade - parity
    half, _, rows, orbits, _ = pieces[0].shape
    eye = unit(orbits)
    for r in range(half):
        right = []
        for relative, piece in enumerate(pieces):
            turn = ((relative // 2) % half) ^ r
            for row in range(rows):
                right.append(jnp.concatenate([piece[turn, 0, row], piece[turn, 1, row]], axis=1))
        total = jnp.dot(
            left[...], jnp.concatenate(right, axis=0), preferred_element_type=jnp.float32
        )
        for row in range(rows):
            mine = colour[domain * own + shade * rows + row] ^ base
            high = total[2 * row * orbits : (2 * row + 1) * orbits]
            low = total[(2 * row + 1) * orbits : (2 * row + 2) * orbits]
            product = high + low
            for q in range(2):
                first = pieces[0][r, q, row].astype(jnp.float32)
                relative = 2 * (r + (half if upper_half else 0)) + q
                probe = jnp.where(mine == relative, eye, 0.0)
                applied = product[:, q * orbits : (q + 1) * orbits] - CENTRE * first
                applied = applied * (1.0 / HALF_WIDTH)
                images[2 * r + (parity ^ q), row] = (
                    coeffs[0] * probe + coeffs[1] * first + coeffs[2] * (2.0 * applied - probe)
                )


def image_terms(coeffs, upper_half, own, colour, left, pieces):
    half, _, rows, orbits, _ = pieces[0].shape
    images = like((2 * half, rows, orbits, orbits), jnp.float32)
    return call(
        functools.partial(image_kernel, coeffs, upper_half, own),
        "image_terms",
        [SMEM] + [VMEM] * (1 + len(pieces)),
        [images],
        [],
        [colour, left, *pieces],
        4,
        1000,
    )[0]


def final_kernel(scale, count, mine, *refs):
    images, refs = refs[: count - 1], refs[count - 1 :]
    blocks, refs = refs[:count], refs[count:]
    firsts, (out, value, sems) = refs[:-3], refs[-3:]
    shade = lax.axis_index("col")
    rows, wide, orbits, _ = blocks[0].shape
    width = wide // 2
    right = []
    for e in range(wide):
        side, i = divmod(e, width)
        first = firsts[side][0, i].astype(jnp.float32)
        for other in firsts[2:]:
            first += other[1 - side, i].astype(jnp.float32)
        right.append(first.astype(jnp.bfloat16))
    right = jnp.concatenate(right + right, axis=0)
    copies = []
    for relative in range(count):
        left = [
            jnp.concatenate([blocks[relative][row, e] for row in range(rows)], axis=0)
            for e in range(wide)
        ]
        left = jnp.concatenate(left, axis=1)
        high = left.astype(jnp.bfloat16)
        low = (left - high.astype(jnp.float32)).astype(jnp.bfloat16)
        extra = jnp.dot(
            jnp.concatenate([high, low], axis=1), right, preferred_element_type=jnp.float32
        )
        if relative == 0:
            image = mine[0]
        else:
            image = images[relative - 1][...] * (1.0 / WIRE_SCALE)
        value[relative] = image.reshape(rows * orbits, orbits) + scale * extra
        at = pl.multiple_of((shade ^ relative) * (rows * orbits), rows * orbits)
        copy = pltpu.make_async_copy(
            value.at[relative], out.at[pl.ds(at, rows * orbits)], sems.at[relative]
        )
        copy.start()
        copies.append(copy)
    for copy in copies:
        copy.wait()


def final_images(scale, mine, images, blocks, firsts):
    count = len(blocks)
    rows, _, orbits, _ = blocks[0].shape
    size = rows * orbits
    return call(
        functools.partial(final_kernel, scale, count),
        "final_images",
        [VMEM] * (1 + len(images) + len(blocks) + len(firsts)),
        [like((count * size, orbits), jnp.float32)],
        [like((count, size, orbits), jnp.float32), pltpu.SemaphoreType.DMA((count,))],
        [mine, *images, *blocks, *firsts],
        4,
        out_space=HBM,
    )[0]


def per_device(ndomain, ncolour, margin, neighbours, pattern, colour, send_list):
    coeffs = cheb_coefficients()
    pairs = ncolour // 2
    half = pairs // 2
    sends = jnp.transpose(send_list, (1, 2, 0))
    rows, width = margin.shape[0], send_list.shape[2]
    own = neighbours.shape[0]

    def across(value, step):
        return lax.ppermute(value, "col", [(i, i ^ step) for i in range(ncolour)])

    near, far, sums = first_terms(ndomain, ncolour, neighbours, pattern, colour, sends, margin)
    border = sums[:, own : own + 2 * width]
    wire = border.astype(WIRE)
    nears, fars, wires = {0: near}, {0: far}, {0: wire}
    nears[1] = across(near, 1)
    fars[1] = across(far, 1)
    near_out, far_out = near, far
    for s in range(1, pairs):
        nears[2 * s] = across(near_out, 2 * s)
        fars[2 * s] = across(far_out, 2 * s)
    up, down = borders(sends, near, far, nears[1], fars[1])
    onward = [(i, (i + 1) % ndomain) for i in range(ndomain)]
    before = lax.ppermute(up, "dom", onward)
    after = lax.ppermute(down, "dom", [(j, i) for i, j in onward])
    for s in range(1, pairs):
        wires[2 * s] = across(wire, 2 * s)
    left = split_sums(own, sums)
    for s in range(1, pairs):
        nears[2 * s], _, _ = lax.optimization_barrier((nears[2 * s], up, down))
        nears[2 * s + 1] = across(nears[2 * s], 1)
    for s in range(1, pairs):
        fars[2 * s + 1] = across(fars[2 * s], 1)

    def pieces(upper):
        picked = []
        for relative in range(ncolour):
            top = relative // 2 >= half
            picked.append((nears if top == upper else fars)[relative])
        return picked

    outer = image_terms(coeffs, True, own, colour, left, pieces(True))
    before, after, outer = lax.optimization_barrier((before, after, outer))
    others = across(jnp.concatenate([wires[2 * s] for s in range(pairs)]), 1)
    for s in range(pairs):
        wires[2 * s + 1] = others[s * rows : (s + 1) * rows]
    blocks = [border] + [wires[m].astype(jnp.float32) for m in range(1, ncolour)]
    images = {}
    sent = (outer * WIRE_SCALE).astype(WIRE)
    for m in range(pairs, ncolour):
        images[m] = sent[m - pairs]
    inner = image_terms(coeffs, False, own, colour, left, pieces(False))
    sent = (inner * WIRE_SCALE).astype(WIRE)
    for m in range(1, pairs):
        images[m] = sent[m]
    firsts = [before, after]
    for m in images:
        if m % 2:
            images[m] = across(images[m], m)
        else:
            second = jnp.stack([after[m // 2], before[m // 2]]).astype(WIRE)
            sent = jnp.concatenate([images[m], second.reshape((-1,) + images[m].shape[1:])])
            sent = across(sent, m)
            images[m], second = sent[:rows], sent[rows:]
            firsts.append(second.reshape((2, width) + second.shape[1:]).astype(jnp.bfloat16))
    return final_images(
        2.0 * coeffs[2] / HALF_WIDTH,
        inner,
        [images[m].astype(jnp.float32) for m in range(1, ncolour)],
        blocks,
        firsts,
    )


def solution(mesh):
    placed = (P(("dom", "col"), None, None, None), P("dom", None), P("dom", None), P(), P())
    return jax.shard_map(
        functools.partial(per_device, mesh.shape["dom"], mesh.shape["col"]),
        mesh=mesh,
        in_specs=placed,
        out_specs=P("dom", "col"),
        check_vma=False,
    )
```

```python
import functools
import math

import jax
import jax.numpy as jnp
from jax import lax
from jax.experimental import pallas as pl
from jax.experimental.pallas import tpu as pltpu
from jax.sharding import PartitionSpec as P

CENTRE = 1.0
HALF_WIDTH = 0.9
HBM = pl.BlockSpec(memory_space=pltpu.HBM)
SMEM = pl.BlockSpec(memory_space=pltpu.SMEM)
VMEM = pl.BlockSpec(memory_space=pltpu.VMEM)
WIRE = jnp.float16
WIRE_SCALE = 0.5
CHUNK = 9


def cheb_coefficients():
    samples = []
    for index_k in range(3):
        angle_value = math.pi * (index_k + 0.5) / 3.0
        samples.append((angle_value, (CENTRE + HALF_WIDTH * math.cos(angle_value)) ** (-0.5)))
    coeffs = []
    for order in range(3):
        coeffs.append(
            2.0
            / 3.0
            * sum((value * math.cos(order * angle_value) for angle_value, value in samples))
        )
    coeffs[0] = 0.5 * coeffs[0]
    return coeffs


def unit(orbits):
    down = lax.broadcasted_iota(jnp.int32, (orbits, orbits), 0)
    along = lax.broadcasted_iota(jnp.int32, (orbits, orbits), 1)
    return (down == along).astype(jnp.float32)


def like(shape, dtype):
    return jax.ShapeDtypeStruct(shape, dtype)


def call(kernel, name, ins, outs, scratch, args, extra=2, cost=1000, out_space=VMEM):
    held = [*outs, *(s for s in scratch if isinstance(s, jax.ShapeDtypeStruct))]
    held += [a for spec, a in zip(ins, args) if spec is VMEM]
    total = sum(math.prod(s.shape) * jnp.dtype(s.dtype).itemsize for s in held)
    return pl.pallas_call(
        kernel,
        out_shape=tuple(outs),
        in_specs=ins,
        out_specs=(out_space,) * len(outs),
        scratch_shapes=[
            pltpu.VMEM(s.shape, s.dtype) if isinstance(s, jax.ShapeDtypeStruct) else s
            for s in scratch
        ],
        compiler_params=pltpu.CompilerParams(vmem_limit_bytes=total + (extra << 20)),
        cost_estimate=pl.CostEstimate(flops=cost, bytes_accessed=1000, transcendentals=0),
        name=name,
    )(*args)


def first_kernel(ndomain, ncolour, *refs):
    tables, margin = refs[:4], refs[4]
    near, far, sums, blocks, totals = refs[5:10]
    neighbours, pattern, colour, sends, table, sems, small = refs[10:]
    domain = lax.axis_index("dom")
    shade = lax.axis_index("col")
    rows, slots, orbits, _ = margin.shape
    own = neighbours.shape[0]
    width = sends.shape[1]
    loads = [
        pltpu.make_async_copy(source, target, small.at[i])
        for i, (source, target) in enumerate(zip(tables, (neighbours, pattern, colour, sends)))
    ]
    for load in loads:
        load.start()
    copies = []
    for row in range(rows):
        for i, k in enumerate(range(0, slots, CHUNK)):
            part = pl.ds(k, min(CHUNK, slots - k))
            copies.append(
                pltpu.make_async_copy(margin.at[row, part], blocks.at[row, part], sems.at[row, i])
            )
    for copy in copies:
        copy.start()
    sums[...] = jnp.zeros_like(sums)
    totals[...] = jnp.zeros_like(totals)
    base = shade - lax.rem(shade, 2)
    lower = lax.rem(domain + ndomain - 1, ndomain)
    upper = lax.rem(domain + 1, ndomain)
    for load in loads:
        load.wait()
    for i in range(own):
        table[i] = colour[domain * own + i] ^ base
    for i in range(width):
        table[own + i] = colour[lower * own + sends[1, i, lower]] ^ base
        table[own + width + i] = colour[upper * own + sends[0, i, upper]] ^ base
    eye = unit(orbits)
    half = ncolour // 4
    for row in range(rows):
        block = shade * rows + row
        totals[row, table[block]] = (-CENTRE) * eye
        for k0 in range(0, slots, CHUNK):
            copies.pop(0).wait()

            @pl.loop(k0, min(k0 + CHUNK, slots), unroll=9)
            def _(k):
                entry = jnp.where(pattern[block, k] == 1, neighbours[block, k], own + 2 * width)
                sums[row, entry] += blocks[row, k].astype(jnp.float32)

        @pl.loop(0, own + 2 * width, unroll=5)
        def _(entry):
            totals[row, table[entry]] += sums[row, entry]

        for c in range(ncolour):
            r = c // 2
            (near if r < half else far)[r % half, c % 2, row] = (
                totals[row, c] * (1.0 / HALF_WIDTH)
            ).astype(jnp.bfloat16)


def first_terms(ndomain, ncolour, neighbours, pattern, colour, sends, margin):
    rows, slots, orbits, _ = margin.shape
    ext = neighbours.shape[0] + 2 * sends.shape[1]
    half = like((ncolour // 4, 2, rows, orbits, orbits), jnp.bfloat16)
    sums = like((rows, ext + 1, orbits, orbits), jnp.float32)
    tables = [neighbours, pattern, colour, sends]
    return call(
        functools.partial(first_kernel, ndomain, ncolour),
        "first_terms",
        [HBM] * 5,
        [half, half, sums],
        [
            like(margin.shape, margin.dtype),
            like((rows, ncolour, orbits, orbits), jnp.float32),
            *[pltpu.SMEM(t.shape, jnp.int32) for t in tables],
            pltpu.SMEM((ext,), jnp.int32),
            pltpu.SemaphoreType.DMA((rows, pl.cdiv(slots, CHUNK))),
            pltpu.SemaphoreType.DMA((4,)),
        ],
        [pltpu.with_memory_space_constraint(t, pltpu.HBM) for t in tables + [margin]],
    )


def border_kernel(sends, near0, far0, near1, far1, up, down):
    domain = lax.axis_index("dom")
    shade = lax.axis_index("col")
    parity = lax.rem(shade, 2)
    half, _, rows, orbits, _ = near0.shape
    for side, out in ((1, up), (0, down)):
        for i in range(sends.shape[1]):
            entry = sends[side, i, domain]
            relative = lax.div(entry, rows) ^ shade
            row = lax.rem(entry, rows)

            @pl.when(relative == 0)
            def _():
                for s in range(2 * half):
                    out[s, i] = (near0 if s < half else far0)[s % half, parity, row]

            @pl.when(relative == 1)
            def _():
                for s in range(2 * half):
                    out[s, i] = (near1 if s < half else far1)[s % half, parity, row]

            @pl.when(relative > 1)
            def _():
                for s in range(2 * half):
                    out[s, i] = jnp.zeros(out.shape[2:], out.dtype)


def borders(sends, near0, far0, near1, far1):
    half, _, _, orbits, _ = near0.shape
    out = like((2 * half, sends.shape[1], orbits, orbits), jnp.bfloat16)
    return call(
        border_kernel,
        "borders",
        [SMEM] + [VMEM] * 4,
        [out, out],
        [],
        [sends, near0, far0, near1, far1],
        cost=1000,
    )


def split_kernel(own, sums, left):
    shade = lax.axis_index("col")
    rows, _, orbits, _ = sums.shape
    for spot in range(own):
        entry = ((spot // rows) ^ shade) * rows + spot % rows
        for row in range(rows):
            value = sums[row, entry]
            high = value.astype(jnp.bfloat16)
            low = (value - high.astype(jnp.float32)).astype(jnp.bfloat16)
            lanes = slice(spot * orbits, (spot + 1) * orbits)
            left[2 * row * orbits : (2 * row + 1) * orbits, lanes] = high
            left[(2 * row + 1) * orbits : (2 * row + 2) * orbits, lanes] = low


def split_sums(own, sums):
    rows, _, orbits, _ = sums.shape
    left = like((2 * rows * orbits, own * orbits), jnp.bfloat16)
    return call(
        functools.partial(split_kernel, own), "split_sums", [VMEM], [left], [], [sums], cost=1000
    )[0]


def image_kernel(coeffs, upper_half, own, colour, left, *refs):
    pieces, images = refs[:-1], refs[-1]
    domain = lax.axis_index("dom")
    shade = lax.axis_index("col")
    parity = lax.rem(shade, 2)
    base = shade - parity
    half, _, rows, orbits, _ = pieces[0].shape
    eye = unit(orbits)
    for r in range(half):
        right = []
        for relative, piece in enumerate(pieces):
            turn = ((relative // 2) % half) ^ r
            for row in range(rows):
                right.append(jnp.concatenate([piece[turn, 0, row], piece[turn, 1, row]], axis=1))
        right = jnp.concatenate(right, axis=0)
        for row in range(rows):
            mine = colour[domain * own + shade * rows + row] ^ base
            both = left[2 * row * orbits : (2 * row + 2) * orbits, :]
            total = jnp.dot(both, right, preferred_element_type=jnp.float32)
            product = total[:orbits] + total[orbits:]
            for q in range(2):
                first = pieces[0][r, q, row].astype(jnp.float32)
                relative = 2 * (r + (half if upper_half else 0)) + q
                probe = jnp.where(mine == relative, eye, 0.0)
                applied = product[:, q * orbits : (q + 1) * orbits] - CENTRE * first
                applied = applied * (1.0 / HALF_WIDTH)
                images[2 * r + (parity ^ q), row] = (
                    coeffs[0] * probe + coeffs[1] * first + coeffs[2] * (2.0 * applied - probe)
                )


def image_terms(coeffs, upper_half, own, colour, left, pieces):
    half, _, rows, orbits, _ = pieces[0].shape
    images = like((2 * half, rows, orbits, orbits), jnp.float32)
    return call(
        functools.partial(image_kernel, coeffs, upper_half, own),
        "image_terms",
        [SMEM] + [VMEM] * (1 + len(pieces)),
        [images],
        [],
        [colour, left, *pieces],
        4,
        1000,
    )[0]


def final_kernel(scale, count, mine, *refs):
    images, refs = refs[: count - 1], refs[count - 1 :]
    blocks, refs = refs[:count], refs[count:]
    firsts, (out, value, sems) = refs[:-3], refs[-3:]
    shade = lax.axis_index("col")
    rows, wide, orbits, _ = blocks[0].shape
    width = wide // 2
    right = []
    for e in range(wide):
        side, i = divmod(e, width)
        first = firsts[side][0, i].astype(jnp.float32)
        for other in firsts[2:]:
            first += other[1 - side, i].astype(jnp.float32)
        right.append(first.astype(jnp.bfloat16))
    right = jnp.concatenate(right + right, axis=0)
    copies = []
    for relative in range(count):
        left = [
            jnp.concatenate([blocks[relative][row, e] for row in range(rows)], axis=0)
            for e in range(wide)
        ]
        left = jnp.concatenate(left, axis=1)
        high = left.astype(jnp.bfloat16)
        low = (left - high.astype(jnp.float32)).astype(jnp.bfloat16)
        extra = jnp.dot(
            jnp.concatenate([high, low], axis=1), right, preferred_element_type=jnp.float32
        )
        if relative == 0:
            image = mine[0]
        else:
            image = images[relative - 1][...] * (1.0 / WIRE_SCALE)
        value[relative] = image.reshape(rows * orbits, orbits) + scale * extra
        at = pl.multiple_of((shade ^ relative) * (rows * orbits), rows * orbits)
        copy = pltpu.make_async_copy(
            value.at[relative], out.at[pl.ds(at, rows * orbits)], sems.at[relative]
        )
        copy.start()
        copies.append(copy)
    for copy in copies:
        copy.wait()


def final_images(scale, mine, images, blocks, firsts):
    count = len(blocks)
    rows, _, orbits, _ = blocks[0].shape
    size = rows * orbits
    return call(
        functools.partial(final_kernel, scale, count),
        "final_images",
        [VMEM] * (1 + len(images) + len(blocks) + len(firsts)),
        [like((count * size, orbits), jnp.float32)],
        [like((count, size, orbits), jnp.float32), pltpu.SemaphoreType.DMA((count,))],
        [mine, *images, *blocks, *firsts],
        4,
        out_space=HBM,
    )[0]


def per_device(ndomain, ncolour, margin, neighbours, pattern, colour, send_list):
    coeffs = cheb_coefficients()
    pairs = ncolour // 2
    half = pairs // 2
    sends = jnp.transpose(send_list, (1, 2, 0))
    rows, width = margin.shape[0], send_list.shape[2]
    own = neighbours.shape[0]

    def across(value, step):
        return lax.ppermute(value, "col", [(i, i ^ step) for i in range(ncolour)])

    near, far, sums = first_terms(ndomain, ncolour, neighbours, pattern, colour, sends, margin)
    border = sums[:, own : own + 2 * width]
    wire = border.astype(WIRE)
    nears, fars, wires = {0: near}, {0: far}, {0: wire}
    nears[1] = across(near, 1)
    fars[1] = across(far, 1)
    near_out, far_out = near, far
    for s in range(1, pairs):
        nears[2 * s] = across(near_out, 2 * s)
        fars[2 * s] = across(far_out, 2 * s)
    up, down = borders(sends, near, far, nears[1], fars[1])
    onward = [(i, (i + 1) % ndomain) for i in range(ndomain)]
    before = lax.ppermute(up, "dom", onward)
    after = lax.ppermute(down, "dom", [(j, i) for i, j in onward])
    for s in range(1, pairs):
        wires[2 * s] = across(wire, 2 * s)
    left = split_sums(own, sums)
    for s in range(1, pairs):
        nears[2 * s], _, _ = lax.optimization_barrier((nears[2 * s], up, down))
        nears[2 * s + 1] = across(nears[2 * s], 1)
    for s in range(1, pairs):
        fars[2 * s + 1] = across(fars[2 * s], 1)

    def pieces(upper):
        picked = []
        for relative in range(ncolour):
            top = relative // 2 >= half
            picked.append((nears if top == upper else fars)[relative])
        return picked

    outer = image_terms(coeffs, True, own, colour, left, pieces(True))
    before, after, outer = lax.optimization_barrier((before, after, outer))
    others = across(jnp.concatenate([wires[2 * s] for s in range(pairs)]), 1)
    for s in range(pairs):
        wires[2 * s + 1] = others[s * rows : (s + 1) * rows]
    blocks = [border] + [wires[m].astype(jnp.float32) for m in range(1, ncolour)]
    images = {}
    sent = (outer * WIRE_SCALE).astype(WIRE)
    for m in range(pairs, ncolour):
        images[m] = sent[m - pairs]
    inner = image_terms(coeffs, False, own, colour, left, pieces(False))
    sent = (inner * WIRE_SCALE).astype(WIRE)
    for m in range(1, pairs):
        images[m] = sent[m]
    firsts = [before, after]
    for m in images:
        if m % 2:
            images[m] = across(images[m], m)
        else:
            second = jnp.stack([after[m // 2], before[m // 2]]).astype(WIRE)
            sent = jnp.concatenate([images[m], second.reshape((-1,) + images[m].shape[1:])])
            sent = across(sent, m)
            images[m], second = sent[:rows], sent[rows:]
            firsts.append(second.reshape((2, width) + second.shape[1:]).astype(jnp.bfloat16))
    return final_images(
        2.0 * coeffs[2] / HALF_WIDTH,
        inner,
        [images[m].astype(jnp.float32) for m in range(1, ncolour)],
        blocks,
        firsts,
    )


def solution(mesh):
    placed = (P(("dom", "col"), None, None, None), P("dom", None), P("dom", None), P(), P())
    return jax.shard_map(
        functools.partial(per_device, mesh.shape["dom"], mesh.shape["col"]),
        mesh=mesh,
        in_specs=placed,
        out_specs=P("dom", "col"),
        check_vma=False,
    )
```
